32 devices in a mesh: row: 8 (over z, x), col: 4 (over y, core).
Axes of the slice: x: 2, y: 2, z: 4, core: 2. Of those that a mesh axis runs over, the one named last changes fastest.
Arguments:
- receptance: bfloat16 [2, 16384, 16384], P(None, 'row', 'col'), may hold values from -4 to 60, as said below
- coupling: int32 [2, 768], replicated, may hold values from 0 to 16383, as said below
Outputs:
- coupled: bfloat16 [2, 16384, 16384], P(None, 'row', 'col')
The draws below stay inside these ranges and needn't reach their ends.
Inputs may be any that keep to these rules, and one draw needn't show every extreme that they name: `coupling`: row 0 holds 768 distinct body DOFs, all in the first half of the 16384 DOFs; row 1 holds 768 distinct cavity DOFs, all in the second half. `receptance`: the driving-point entry of every body or cavity DOF named in coupling (same response and excitation DOF) has real part 52 or more; every other real or imaginary part lies within -4 to 4.
All inputs are finite; a program needn't handle non-finite values.
Results may differ from the reference program's by a relative error of at most 0.015.
Values may be sent and summed in bfloat16 or wider, within the bound.
A program may use at most 320 MiB of HBM per device.

```python
import jax
import jax.numpy as jnp
from jax import lax

NDOF = 16384
NI = 768
SWEEPS = 6


def pair_table(key):
    base = jax.random.fold_in(key, 7)
    first_key, second_key = jax.random.split(base)
    body_list = jax.random.permutation(first_key, NDOF // 2)[:NI]
    cavity_list = NDOF // 2 + jax.random.permutation(second_key, NDOF // 2)[:NI]
    return jnp.stack([body_list, cavity_list]).astype(jnp.int32)


def draw_coupling(key, part):
    return pair_table(key)


def draw_receptance(key, part):
    pairs = pair_table(key)
    value_key = jax.random.fold_in(key, 11)
    values = jax.random.truncated_normal(value_key, -4.0, 4.0, (2, NDOF, NDOF), jnp.float32)
    marked = pairs.reshape(-1)
    values = values.at[0, marked, marked].add(56.0)
    return values.astype(jnp.bfloat16)


def setup_inputs(seed: int = 0) -> dict:
    key_of = jax.random.split(jax.random.key(seed), 3)
    receptance = draw_receptance(jax.random.fold_in(key_of[2], 71), 0)
    coupling = draw_coupling(jax.random.fold_in(key_of[2], 71), 0)
    return {"receptance": receptance, "coupling": coupling}


def complex_times(mat_real, mat_imag, vec_real, vec_imag):
    hi = lax.Precision.HIGHEST
    out_real = jnp.dot(mat_real, vec_real, precision=hi) - jnp.dot(mat_imag, vec_imag, precision=hi)
    out_imag = jnp.dot(mat_real, vec_imag, precision=hi) + jnp.dot(mat_imag, vec_real, precision=hi)
    return out_real, out_imag


def reference(receptance, coupling):
    body_dof = coupling[0]
    cav_dof = coupling[1]
    rhs = receptance[:, body_dof, :].astype(jnp.float32) - receptance[:, cav_dof, :].astype(jnp.float32)
    left_full = receptance[:, :, body_dof].astype(jnp.float32) - receptance[:, :, cav_dof].astype(jnp.float32)
    left = left_full.astype(jnp.bfloat16)
    interface = rhs[:, :, body_dof] - rhs[:, :, cav_dof]
    z_real = interface[0]
    z_imag = interface[1]
    diag_real = jnp.diagonal(z_real)
    diag_imag = jnp.diagonal(z_imag)
    modulus = diag_real * diag_real + diag_imag * diag_imag
    d_real = (diag_real / modulus)[:, None]
    d_imag = (-diag_imag / modulus)[:, None]

    def scale(part_real, part_imag):
        return d_real * part_real - d_imag * part_imag, d_real * part_imag + d_imag * part_real

    v_real = rhs[0]
    v_imag = rhs[1]
    x_real, x_imag = scale(v_real, v_imag)
    for sweep_index in range(SWEEPS):
        p_real, p_imag = complex_times(z_real, z_imag, x_real, x_imag)
        e_real, e_imag = scale(v_real - p_real, v_imag - p_imag)
        x_real = x_real + e_real
        x_imag = x_imag + e_imag
    w_real = x_real.astype(jnp.bfloat16)
    w_imag = x_imag.astype(jnp.bfloat16)
    block_rows = NDOF // 16
    left_blocks = left.reshape(2, 16, block_rows, NI).transpose(1, 0, 2, 3)
    recv_blocks = receptance.reshape(2, 16, block_rows, NDOF).transpose(1, 0, 2, 3)

    def one_block(pair):
        left_block, recv_block = pair
        u_real = left_block[0]
        u_imag = left_block[1]
        c_real = jnp.dot(u_real, w_real, preferred_element_type=jnp.float32) - jnp.dot(u_imag, w_imag, preferred_element_type=jnp.float32)
        c_imag = jnp.dot(u_real, w_imag, preferred_element_type=jnp.float32) + jnp.dot(u_imag, w_real, preferred_element_type=jnp.float32)
        corr = jnp.stack([c_real, c_imag])
        return (recv_block.astype(jnp.float32) - corr).astype(jnp.bfloat16)

    outs = lax.map(one_block, (left_blocks, recv_blocks))
    return outs.transpose(1, 0, 2, 3).reshape(2, NDOF, NDOF)
```

```python
import functools

import jax
import jax.numpy as jnp
from jax import lax
from jax.experimental import pallas as pl
from jax.experimental.pallas import tpu as pltpu
from jax.sharding import PartitionSpec as P

BF = jnp.bfloat16
F32 = jnp.float32


def signed_table(body_dof, cav_dof, offset, extent):
    positions = offset + lax.broadcasted_iota(jnp.int32, (extent, 1), 0)
    table = (positions == body_dof[None, :]).astype(F32) - (positions == cav_dof[None, :]).astype(F32)
    return table.astype(BF)


def signed_table_t(body_dof, cav_dof, offset, extent):
    positions = offset + lax.broadcasted_iota(jnp.int32, (1, extent), 1)
    table = (positions == body_dof[:, None]).astype(F32) - (positions == cav_dof[:, None]).astype(F32)
    return table.astype(BF)


def sum_over_col(x, size):
    if size < 2 or size & (size - 1) or x.shape[1] % 32:
        return lax.psum(x, "col")
    half = x.shape[1] // 2
    me = lax.axis_index("col")
    bit = me % 2
    pair = [(i, i ^ 1) for i in range(size)]
    mine = lax.dynamic_slice_in_dim(x, bit * half, half, 1)
    other = lax.dynamic_slice_in_dim(x, (1 - bit) * half, half, 1)
    mine = mine + lax.ppermute(other, "col", pair)
    step = 2
    while step < size:
        mine = mine + lax.ppermute(mine, "col", [(i, i ^ step) for i in range(size)])
        step *= 2
    other = lax.ppermute(mine, "col", pair)
    low = jnp.where(bit == 0, mine, other)
    high = jnp.where(bit == 0, other, mine)
    return jnp.concatenate([low, high], axis=1)


def final_kernel(first, *refs):
    if first:
        y_ref, u_ref, w_ref, o_ref = refs
    else:
        y_ref, u_ref, w_ref, _, o_ref = refs
    for p in range(2):
        c = jnp.dot(u_ref[p], w_ref[...], preferred_element_type=F32)
        o_ref[p] = (y_ref[p].astype(F32) - c).astype(BF)


def final_chunk(y, u, w, prev, index):
    _, rows, cols = y.shape
    depth, width = w.shape
    bm = min(512, rows)
    bn = min(1024, width)
    base = index * (width // bn)
    first = prev is None
    in_specs = [
        pl.BlockSpec((2, bm, bn), lambda j, i: (0, i, base + j)),
        pl.BlockSpec((2, bm, depth), lambda j, i: (0, i, 0)),
        pl.BlockSpec((depth, bn), lambda j, i: (0, j)),
    ]
    args = [y, u, w]
    aliases = {}
    if not first:
        in_specs.append(pl.BlockSpec(memory_space=pl.ANY))
        args.append(prev)
        aliases = {3: 0}
    return pl.pallas_call(
        functools.partial(final_kernel, first),
        grid=(width // bn, rows // bm),
        in_specs=in_specs,
        out_specs=pl.BlockSpec((2, bm, bn), lambda j, i: (0, i, base + j)),
        out_shape=jax.ShapeDtypeStruct(y.shape, BF),
        input_output_aliases=aliases,
        compiler_params=pltpu.CompilerParams(vmem_limit_bytes=48 * 1024 * 1024),
        cost_estimate=pl.CostEstimate(
            flops=4 * rows * depth * width,
            bytes_accessed=8 * rows * width + 4 * rows * depth + 2 * depth * width,
            transcendentals=0,
        ),
    )(*args)


def times(a_r, a_i, b_r, b_i, precision=lax.Precision.HIGH):
    left = jnp.concatenate([a_r, a_i], axis=1)
    right = jnp.concatenate(
        [jnp.concatenate([b_r, b_i], axis=1), jnp.concatenate([-b_i, b_r], axis=1)], axis=0
    )
    out = jnp.dot(left, right, precision=precision, preferred_element_type=F32)
    n = b_r.shape[1]
    return out[:, :n], out[:, n:]


def solve_operator(z_real, z_imag):
    n = z_real.shape[0]
    eye = lax.broadcasted_iota(jnp.int32, (n, n), 0) == lax.broadcasted_iota(jnp.int32, (n, n), 1)
    zero = jnp.zeros((), F32)

    def inverse(axis):
        re = jnp.sum(jnp.where(eye, z_real, zero), axis=axis, keepdims=True)
        im = jnp.sum(jnp.where(eye, z_imag, zero), axis=axis, keepdims=True)
        modulus = re * re + im * im
        return re / modulus, -im / modulus

    d_r, d_i = inverse(1)
    o_r = jnp.where(eye, zero, z_real)
    o_i = jnp.where(eye, zero, z_imag)
    a_r = -(d_r * o_r - d_i * o_i)
    a_i = -(d_r * o_i + d_i * o_r)
    s_r, s_i = times(a_r, a_i, a_r, a_i)
    q_r, q_i = times(s_r, s_i, s_r, s_i)
    one = eye.astype(F32)
    p_r, p_i = times(a_r + s_r, a_i + s_i, one + s_r + q_r, s_i + q_i)
    p_r = p_r + one
    e_r, e_i = inverse(0)
    w_r = p_r * e_r - p_i * e_i
    w_i = p_r * e_i + p_i * e_r
    first = jnp.concatenate(
        [jnp.concatenate([w_r, -w_i], axis=1), jnp.concatenate([-w_i, -w_r], axis=1)], axis=0
    )
    second = jnp.concatenate(
        [jnp.concatenate([w_i, w_r], axis=1), jnp.concatenate([w_r, -w_i], axis=1)], axis=0
    )
    return jnp.stack([first, second]).astype(BF)


def local(row_size, col_size, receptance, coupling):
    _, tile_rows, tile_cols = receptance.shape
    row_index = lax.axis_index("row")
    col_index = lax.axis_index("col")
    body_dof = coupling[0]
    cav_dof = coupling[1]
    count = body_dof.shape[0]
    col_table = signed_table(body_dof, cav_dof, col_index * tile_cols, tile_cols)
    row_table = signed_table_t(body_dof, cav_dof, row_index * tile_rows, tile_rows)

    chunks = 4 if tile_cols % 512 == 0 else 1
    width = tile_cols // chunks

    def row_chunk(j, table):
        part = receptance[:, :, j * width : (j + 1) * width]
        terms = jnp.einsum("nr,prc->pnc", table, part, preferred_element_type=F32).astype(BF)
        return terms.reshape(2 * count, width)

    def scatter(terms):
        return lax.psum_scatter(terms, "row", scatter_dimension=0, tiled=True)

    rows = row_chunk(0, row_table)
    col_table, rows = lax.optimization_barrier((col_table, rows))
    scattered = [scatter(rows)]
    col_terms = jnp.einsum("prc,cn->prn", receptance, col_table, preferred_element_type=F32).astype(BF)
    inter_terms = jnp.einsum("mr,prn->pmn", row_table, col_terms, preferred_element_type=F32).astype(BF)
    interface = lax.psum(inter_terms, ("row", "col"))
    scattered += [scatter(row_chunk(j, row_table)) for j in range(1, chunks)]
    left = sum_over_col(col_terms, col_size)
    z = interface.astype(F32)
    pages = solve_operator(z[0], z[1])
    left = jnp.concatenate([left[0], left[1]], axis=1)
    u = jnp.einsum("rk,pkn->prn", left, pages, preferred_element_type=F32).astype(BF)
    out = None
    for j in range(chunks):
        piece = lax.all_gather(scattered[j], "row", axis=0, tiled=True)
        out = final_chunk(receptance, u, piece, out, j)
    return out


def solution(mesh):
    in_specs = (P(None, "row", "col"), P())
    out_specs = P(None, "row", "col")
    body = functools.partial(local, mesh.shape["row"], mesh.shape["col"])
    return jax.shard_map(body, mesh=mesh, in_specs=in_specs, out_specs=out_specs, check_vma=False)
```

```python
import functools

import jax
import jax.numpy as jnp
from jax import lax
from jax.experimental import pallas as pl
from jax.experimental.pallas import tpu as pltpu
from jax.sharding import PartitionSpec as P

BF = jnp.bfloat16
F32 = jnp.float32


def signed_table(body_dof, cav_dof, offset, extent):
    positions = offset + lax.broadcasted_iota(jnp.int32, (extent, 1), 0)
    table = (positions == body_dof[None, :]).astype(F32) - (positions == cav_dof[None, :]).astype(F32)
    return table.astype(BF)


def signed_table_t(body_dof, cav_dof, offset, extent):
    positions = offset + lax.broadcasted_iota(jnp.int32, (1, extent), 1)
    table = (positions == body_dof[:, None]).astype(F32) - (positions == cav_dof[:, None]).astype(F32)
    return table.astype(BF)


def sum_over_col(x, size):
    if size < 2 or size & (size - 1) or x.shape[1] % 32:
        return lax.psum(x, "col")
    half = x.shape[1] // 2
    me = lax.axis_index("col")
    bit = me % 2
    pair = [(i, i ^ 1) for i in range(size)]
    mine = lax.dynamic_slice_in_dim(x, bit * half, half, 1)
    other = lax.dynamic_slice_in_dim(x, (1 - bit) * half, half, 1)
    mine = mine + lax.ppermute(other, "col", pair)
    step = 2
    while step < size:
        mine = mine + lax.ppermute(mine, "col", [(i, i ^ step) for i in range(size)])
        step *= 2
    other = lax.ppermute(mine, "col", pair)
    low = jnp.where(bit == 0, mine, other)
    high = jnp.where(bit == 0, other, mine)
    return jnp.concatenate([low, high], axis=1)


def final_kernel(first, *refs):
    if first:
        y_ref, u_ref, w_ref, o_ref = refs
    else:
        y_ref, u_ref, w_ref, _, o_ref = refs
    for p in range(2):
        c = jnp.dot(u_ref[p], w_ref[...], preferred_element_type=F32)
        o_ref[p] = (y_ref[p].astype(F32) - c).astype(BF)


def final_chunk(y, u, w, prev, offset):
    _, rows, cols = y.shape
    depth, width = w.shape
    bm = min(512, rows)
    bn = 1024 if width % 1024 == 0 else width
    base = offset // bn
    first = prev is None
    in_specs = [
        pl.BlockSpec((2, bm, bn), lambda j, i: (0, i, base + j)),
        pl.BlockSpec((2, bm, depth), lambda j, i: (0, i, 0)),
        pl.BlockSpec((depth, bn), lambda j, i: (0, j)),
    ]
    args = [y, u, w]
    aliases = {}
    if not first:
        in_specs.append(pl.BlockSpec(memory_space=pl.ANY))
        args.append(prev)
        aliases = {3: 0}
    return pl.pallas_call(
        functools.partial(final_kernel, first),
        grid=(width // bn, rows // bm),
        in_specs=in_specs,
        out_specs=pl.BlockSpec((2, bm, bn), lambda j, i: (0, i, base + j)),
        out_shape=jax.ShapeDtypeStruct(y.shape, BF),
        input_output_aliases=aliases,
        compiler_params=pltpu.CompilerParams(vmem_limit_bytes=48 * 1024 * 1024),
        cost_estimate=pl.CostEstimate(
            flops=4 * rows * depth * width,
            bytes_accessed=8 * rows * width + 4 * rows * depth + 2 * depth * width,
            transcendentals=0,
        ),
    )(*args)


def times(a_r, a_i, b_r, b_i):
    a_r, a_i, b_r, b_i = (x.astype(BF) for x in (a_r, a_i, b_r, b_i))
    left = jnp.concatenate([a_r, a_i], axis=1)
    right = jnp.concatenate(
        [jnp.concatenate([b_r, b_i], axis=1), jnp.concatenate([-b_i, b_r], axis=1)], axis=0
    )
    out = jnp.dot(left, right, preferred_element_type=F32)
    n = b_r.shape[1]
    return out[:, :n], out[:, n:]


def solve_operator(z_real, z_imag):
    n = z_real.shape[0]
    eye = lax.broadcasted_iota(jnp.int32, (n, n), 0) == lax.broadcasted_iota(jnp.int32, (n, n), 1)
    zero = jnp.zeros((), F32)

    def inverse(axis):
        re = jnp.sum(jnp.where(eye, z_real, zero), axis=axis, keepdims=True)
        im = jnp.sum(jnp.where(eye, z_imag, zero), axis=axis, keepdims=True)
        modulus = re * re + im * im
        return re / modulus, -im / modulus

    d_r, d_i = inverse(1)
    o_r = jnp.where(eye, zero, z_real)
    o_i = jnp.where(eye, zero, z_imag)
    a_r = -(d_r * o_r - d_i * o_i)
    a_i = -(d_r * o_i + d_i * o_r)
    s_r, s_i = times(a_r, a_i, a_r, a_i)
    q_r, q_i = times(s_r, s_i, s_r, s_i)
    one = eye.astype(F32)
    p_r, p_i = times(a_r + s_r, a_i + s_i, one + s_r + q_r, s_i + q_i)
    p_r = p_r + one
    e_r, e_i = inverse(0)
    w_r = p_r * e_r - p_i * e_i
    w_i = p_r * e_i + p_i * e_r
    first = jnp.concatenate(
        [jnp.concatenate([w_r, -w_i], axis=1), jnp.concatenate([-w_i, -w_r], axis=1)], axis=0
    )
    second = jnp.concatenate(
        [jnp.concatenate([w_i, w_r], axis=1), jnp.concatenate([w_r, -w_i], axis=1)], axis=0
    )
    return jnp.stack([first, second]).astype(BF)


def local(row_size, col_size, receptance, coupling):
    _, tile_rows, tile_cols = receptance.shape
    row_index = lax.axis_index("row")
    col_index = lax.axis_index("col")
    body_dof = coupling[0]
    cav_dof = coupling[1]
    count = body_dof.shape[0]
    col_table = signed_table(body_dof, cav_dof, col_index * tile_cols, tile_cols)
    row_table = signed_table_t(body_dof, cav_dof, row_index * tile_rows, tile_rows)

    rows = jnp.einsum("nr,prc->pnc", row_table, receptance, preferred_element_type=F32).astype(BF)
    rows = rows.reshape(2 * count, tile_cols)
    col_table, rows = lax.optimization_barrier((col_table, rows))
    rhs = lax.psum_scatter(rows, "row", scatter_dimension=0, tiled=True)
    col_terms = jnp.einsum("prc,cn->prn", receptance, col_table, preferred_element_type=F32).astype(BF)
    inter_terms = jnp.einsum("mr,prn->pmn", row_table, col_terms, preferred_element_type=F32).astype(BF)
    interface = lax.psum(inter_terms, ("row", "col"))
    left = sum_over_col(col_terms, col_size)
    z = interface.astype(F32)
    pages = solve_operator(z[0], z[1])
    left = jnp.concatenate([left[0], left[1]], axis=1)
    u = jnp.einsum("rk,pkn->prn", left, pages, preferred_element_type=F32).astype(BF)
    cut = tile_cols - tile_cols // 4 if tile_cols % 512 == 0 else tile_cols
    out = None
    for start, stop in ((0, cut), (cut, tile_cols)):
        if stop > start:
            piece = lax.all_gather(rhs[:, start:stop], "row", axis=0, tiled=True)
            out = final_chunk(receptance, u, piece, out, start)
    return out


def solution(mesh):
    in_specs = (P(None, "row", "col"), P())
    out_specs = P(None, "row", "col")
    body = functools.partial(local, mesh.shape["row"], mesh.shape["col"])
    return jax.shard_map(body, mesh=mesh, in_specs=in_specs, out_specs=out_specs, check_vma=False)
```
